32 devices in a mesh: expert: 8 (over z, x), tensor: 4 (over y, core).
Axes of the slice: x: 2, y: 2, z: 4, core: 2. Of those that a mesh axis runs over, the one named last changes fastest.
Arguments:
- tokens: bfloat16 [4096, 2048], P('expert'), may hold values from -40 to 40
- norm_gain: float32 [2048], replicated, may hold values from 0.5 to 1.5
- expert_ids: int32 [4096, 8], P('expert'), may hold values from 0 to 31, all different within a row; in each aligned block of 512 rows (0 to 511, 512 to 1023, ...) at most 136 rows name the same one
- route_weights: float32 [4096, 8], P('expert'), may hold values from 0.5 to 1
- w_gate: bfloat16 [32, 2048, 768], P('expert', None, 'tensor'), may hold values from -0.125 to 0.125
- w_up: bfloat16 [32, 2048, 768], P('expert', None, 'tensor'), may hold values from -0.125 to 0.125
- w_down: bfloat16 [32, 768, 2048], P('expert', 'tensor'), may hold values from -0.21875 to 0.21875
- codec_embeds: bfloat16 [8192, 1024], P(('expert', 'tensor')), may hold values from -30 to 30
- frame_lengths: int32 [16], P('expert'), may hold values from 128 to 896, as said below
- source_rows: int32 [8192], P(('expert', 'tensor')), may hold values from 0 to 4095, as said below
- w_handover: bfloat16 [2048, 1024], replicated, may hold values from -0.125 to 0.125
- talker_gain: float32 [1024], replicated, may hold values from 0.5 to 1.5
- w_query: bfloat16 [1024, 1024], replicated, may hold values from -1 to 1
- w_kv: bfloat16 [1024, 1024], replicated, may hold values from -1 to 1
- qk_gains: float32 [2, 128], replicated, may hold values from 1 to 5
- w_out: bfloat16 [1024, 1024], replicated, may hold values from -0.1875 to 0.1875
Outputs:
- thinker_out: bfloat16 [4096, 2048], P(('expert', 'tensor'))
- talker_out: bfloat16 [8192, 1024], P(('expert', 'tensor'))
The draws below stay inside these ranges and needn't reach their ends.
Inputs may be any that keep to these rules, and one draw needn't show every extreme that they name: `expert_ids`: in each aligned block of 512 tokens no expert is named by more than 136 routes, and in every draw some expert is named by exactly 136 routes of some block. `frame_lengths`: entries 2 g and 2 g + 1 are the frame counts of the two dialogues of group g and sum to 1024. `source_rows`: A frame of group g reads one of the thinker rows g * 512 to (g + 1) * 512 - 1; along the frames of one dialogue the rows never fall.
All inputs are finite; a program needn't handle non-finite values.
Results may differ from the reference program's by a relative error of at most 0.04.
Values may be sent and summed in bfloat16 or wider, within the bound.
No kernel may reach another device: no remote copies, remote signals or barrier semaphores. Data moves between devices by JAX's collectives and lax.ppermute only.
A program may use at most 192 MiB of HBM per device.

```python
import math
import jax
import jax.numpy as jnp
import numpy as np
from jax import lax

D = 2048
FF = 768
EXPERTS = 32
TOPK = 8
TOK_DEV = 512
TOKENS = 4096
CAP = 136
FF_PART = 192
TW = 1024
HEADS = 8
KV_HEADS = 4
HEAD = 128
GROUP_FRAMES = 1024
FRAMES = 8192
DIALOGS = 16
N_EXPERT = 8
N_TENSOR = 4


def scaled_rows(key, row_count, col_count, row_lo, row_hi, limit):
    first_key, second_key, third_key = jax.random.split(key, 3)
    base = jax.random.normal(first_key, (row_count, col_count), jnp.float32)
    row_scale = jnp.exp(jax.random.uniform(second_key, (row_count, 1), jnp.float32, math.log(row_lo), math.log(row_hi)))
    col_scale = jnp.exp(jax.random.uniform(third_key, (1, col_count), jnp.float32, math.log(0.5), math.log(2.0)))
    return jnp.clip(base * row_scale * col_scale, -limit, limit)


def draw_tokens(key, part):
    return scaled_rows(jax.random.fold_in(key, 11), TOKENS, D, 0.5, 5.0, 40.0).astype(jnp.bfloat16)


def draw_codec_embeds(key, part):
    return scaled_rows(jax.random.fold_in(key, 13), FRAMES, TW, 0.3, 3.0, 30.0).astype(jnp.bfloat16)


def talker_weights(key):
    base = jax.random.fold_in(key, 31)
    first_key, second_key, third_key = jax.random.split(base, 3)
    scale = TW ** (-0.5)
    queries = jax.random.normal(first_key, (TW, HEADS * HEAD), jnp.float32) * scale
    key_part = jax.random.normal(second_key, (TW, KV_HEADS * HEAD), jnp.float32) * scale
    value_part = jax.random.normal(third_key, (TW, KV_HEADS * HEAD), jnp.float32) * scale
    return (jnp.clip(queries, -1.0, 1.0), jnp.clip(jnp.concatenate([key_part, value_part], axis=1), -1.0, 1.0))


def draw_w_query(key, part):
    return talker_weights(key)[0].astype(jnp.bfloat16)


def draw_w_kv(key, part):
    return talker_weights(key)[1].astype(jnp.bfloat16)


def draw_qk_gains(key, part):
    gain_key = jax.random.fold_in(key, 43)
    return jax.random.uniform(gain_key, (2, HEAD), jnp.float32, 1.0, 1.5)


def frame_plan(key):
    base = jax.random.fold_in(key, 57)
    first_key, second_key, third_key = jax.random.split(base, 3)
    group_count = DIALOGS // 2
    margin = GROUP_FRAMES // 8
    spread = GROUP_FRAMES - 2 * margin
    offset = jax.random.randint(first_key, (group_count,), 0, spread + 1, jnp.int32)
    order = jax.random.permutation(second_key, group_count)
    offset = offset.at[order[0]].set(spread).at[order[1]].set(0)
    first_length = margin + offset
    split_rows = jax.random.randint(third_key, (group_count,), TOK_DEV // 4, 3 * TOK_DEV // 4 + 1, jnp.int32)
    lengths = jnp.stack([first_length, GROUP_FRAMES - first_length], axis=1).reshape(group_count * 2)
    positions = jnp.arange(GROUP_FRAMES, dtype=jnp.int32)[None, :]
    later = positions >= first_length[:, None]
    inner = positions - jnp.where(later, first_length[:, None], 0)
    frame_total = jnp.where(later, GROUP_FRAMES - first_length[:, None], first_length[:, None])
    row_start = jnp.where(later, split_rows[:, None], 0)
    row_span = jnp.where(later, TOK_DEV - split_rows[:, None], split_rows[:, None])
    group_base = jnp.arange(group_count, dtype=jnp.int32)[:, None] * TOK_DEV
    row_index = group_base + row_start + inner * row_span // frame_total
    return (lengths.astype(jnp.int32), row_index.reshape(group_count * GROUP_FRAMES).astype(jnp.int32))


def draw_frame_lengths(key, part):
    return frame_plan(key)[0]


def draw_source_rows(key, part):
    return frame_plan(key)[1]


def block_levels(stream_key, extent, cuts, smallest, largest):
    factor_of = 1.0
    for position, blocks in cuts:
        heights = jax.random.uniform(jax.random.fold_in(jax.random.fold_in(stream_key, 6), position), (blocks,), jnp.float32, smallest / len(cuts), largest / len(cuts))
        factor_of = factor_of * jnp.repeat(jnp.exp(heights), extent[position] // blocks).reshape((-1,) + (1,) * (len(extent) - 1 - position))
    return factor_of


def deal_out(own_key, own, number, rows, count, top, most, lean):
    ranking = jax.random.permutation(own_key, count)
    crowded, ordinary = shares(count, rows * top, most, lean, True), shares(count, rows * top, most, lean, False)
    places = jnp.arange(count)

    def named(sizes, rotation):
        used = int((sizes > 0).sum())
        fixed = max(1, used // 4)
        shifted = fixed + (places - fixed + rotation * (used - fixed)) % max(1, count - fixed)
        return jnp.zeros((count,), jnp.int32).at[ranking[jnp.where(places < fixed, places, shifted)]].set(jnp.asarray(sizes, jnp.int32))

    sizes = jnp.where(number % 4 == 0, named(crowded, number // 4), named(ordinary, number - number // 4 - 1))
    mixed = jax.random.permutation(jax.random.fold_in(own, 3), count)
    source_of, receiver = mixed[0:count // 2 * 2:2], mixed[1:count // 2 * 2:2]
    room = jnp.minimum(sizes[source_of] - 1, most - sizes[receiver]) // 2
    room = jnp.where((source_of == ranking[0]) | (receiver == ranking[0]) | (sizes[receiver] == 0), 0, jnp.maximum(room, 0))
    shifted = jax.random.randint(jax.random.fold_in(own, 4), (count // 2,), 0, 1 << 20) % (room + 1)
    sizes = sizes.at[source_of].add(-shifted).at[receiver].add(shifted)
    members = jnp.searchsorted(jnp.cumsum(sizes), jnp.arange(rows * top), side="right").astype(jnp.int32)
    listing = members.reshape(top, rows).T
    listing = listing[jax.random.permutation(jax.random.fold_in(own, 1), rows)]
    rotation = jax.random.randint(jax.random.fold_in(own, 2), (rows, 1), 0, top)
    return jnp.take_along_axis(listing, (jnp.arange(top)[None, :] + rotation) % top, axis=1)


def shares(amount, total, most, lean, full):
    loads = [(1 << 20) // math.isqrt(standing ** lean) + 1 for standing in range(1, amount + 1)]
    largest = most if full else min(most, max(-(-total // amount), total * loads[0] // sum(loads)))
    least = 1 if total - largest >= amount - 1 else 0
    given, spare = [largest] + [least] * (amount - 1), total - largest - least * (amount - 1)
    while spare > 0:
        candidates = [i for i in range(1, amount) if given[i] < largest] or [i for i in range(1, amount) if given[i] < most]
        whole, remaining = sum([loads[i] for i in candidates]), spare
        for i in candidates:
            more = min(most - given[i], max(1, remaining * loads[i] // whole), spare)
            given[i] = given[i] + more
            spare = spare - more
    return np.array(given)


def normal_values(stream_key, shape, scale, reach, shards=(), kind=jnp.bfloat16):
    entries = scale * jax.random.normal(stream_key, shape, jnp.float32)
    if shards:
        entries = entries * block_levels(stream_key, shape, shards, -0.22, 0.18)
    return jnp.clip(entries, -reach, reach).astype(kind)


def setup_inputs(seed: int = 0) -> dict:
    seeds = jax.random.split(jax.random.key(seed), 17)
    tokens = draw_tokens(jax.random.fold_in(seeds[16], 71), 0)
    norm_gain = jnp.clip(1.0 + 0.1 * jax.random.normal(seeds[1], (D,), jnp.float32), 0.5, 1.5)
    expert_ids_keys = jax.random.split(jax.random.fold_in(seeds[2], 1), TOKENS // TOK_DEV)
    expert_ids_turns = jax.random.permutation(jax.random.fold_in(seeds[2], 3), TOKENS // TOK_DEV)
    expert_ids = jax.vmap(lambda own, number: deal_out(jax.random.fold_in(seeds[2], 2), own, number, TOK_DEV, EXPERTS, TOPK, CAP, 1))(expert_ids_keys, expert_ids_turns).reshape((TOKENS, TOPK))
    route_weights = jnp.clip(0.5 + 0.5 * jax.random.uniform(seeds[3], (TOKENS, TOPK), jnp.float32) ** block_levels(seeds[3], (TOKENS, TOPK), ((0, 8),), -0.2, 0.2), 0.5, 1.0)
    w_gate = normal_values(seeds[4], (EXPERTS, D, FF), D ** -0.5, 0.125, ((0, 8), (2, 4)))
    w_up = normal_values(seeds[5], (EXPERTS, D, FF), D ** -0.5, 0.125, ((0, 8), (2, 4)))
    w_down = normal_values(seeds[6], (EXPERTS, FF, D), FF ** -0.5, 0.21875, ((0, 8), (1, 4)))
    codec_embeds = draw_codec_embeds(jax.random.fold_in(seeds[16], 71), 0)
    frame_lengths = draw_frame_lengths(jax.random.fold_in(seeds[16], 71), 0)
    source_rows = draw_source_rows(jax.random.fold_in(seeds[16], 71), 0)
    w_handover = normal_values(seeds[10], (D, TW), D ** -0.5, 0.125)
    talker_gain = jnp.clip(1.0 + 0.1 * jax.random.normal(seeds[11], (TW,), jnp.float32), 0.5, 1.5)
    w_query = draw_w_query(jax.random.fold_in(seeds[16], 71), 0)
    w_kv = draw_w_kv(jax.random.fold_in(seeds[16], 71), 0)
    qk_gains = draw_qk_gains(jax.random.fold_in(seeds[16], 71), 0)
    w_out = normal_values(seeds[15], (HEADS * HEAD, TW), (HEADS * HEAD) ** -0.5, 0.1875)
    return dict(tokens=tokens, norm_gain=norm_gain, expert_ids=expert_ids, route_weights=route_weights, w_gate=w_gate, w_up=w_up, w_down=w_down, codec_embeds=codec_embeds, frame_lengths=frame_lengths, source_rows=source_rows, w_handover=w_handover, talker_gain=talker_gain, w_query=w_query, w_kv=w_kv, qk_gains=qk_gains, w_out=w_out)


epsilon = 1e-06

def rms_scale(values, gain):
    mean_square = lax.optimization_barrier(jnp.mean(values * values, axis=-1, keepdims=True))
    return values * lax.rsqrt(mean_square + epsilon) * gain

def reference(tokens, norm_gain, expert_ids, route_weights, w_gate, w_up, w_down, codec_embeds, frame_lengths, source_rows, w_handover, talker_gain, w_query, w_kv, qk_gains, w_out):
    normed = rms_scale(tokens.astype(jnp.float32), norm_gain).astype(jnp.bfloat16)
    padded = jnp.concatenate([normed, jnp.zeros((1, D), jnp.bfloat16)], axis=0)
    route_count = TOK_DEV * TOPK
    grouped_ids = expert_ids.reshape(N_EXPERT, route_count)
    one_hot = (grouped_ids[:, :, None] == jnp.arange(EXPERTS, dtype=jnp.int32)[None, None, :]).astype(jnp.int32)
    before = jnp.cumsum(one_hot, axis=1) - one_hot
    slot_rank = lax.optimization_barrier(jnp.sum(before * one_hot, axis=2)).astype(jnp.int32)
    group_ids = jnp.arange(N_EXPERT, dtype=jnp.int32)[:, None]
    anchor = group_ids * TOK_DEV + jnp.arange(route_count, dtype=jnp.int32)[None, :] // TOPK
    column = grouped_ids * (N_EXPERT * CAP) + group_ids * CAP + slot_rank
    route_share = route_weights / lax.optimization_barrier(jnp.sum(route_weights, axis=1, keepdims=True))
    token_table = jnp.full((EXPERTS * N_EXPERT * CAP,), TOKENS, jnp.int32)
    token_table = token_table.at[column.reshape(-1)].set(anchor.reshape(-1))
    weight_table = jnp.zeros((EXPERTS * N_EXPERT * CAP,), jnp.float32)
    weight_table = weight_table.at[column.reshape(-1)].set(route_share.reshape(-1))
    token_table = token_table.reshape(EXPERTS, N_EXPERT * CAP)
    weight_table = weight_table.reshape(EXPERTS, N_EXPERT * CAP)

    def one_expert(mixed, inputs):
        gate_weight, up_weight, down_weight, indices, scales = inputs
        block_rows = padded[indices]
        gate_proj = jnp.dot(block_rows, gate_weight, preferred_element_type=jnp.float32)
        up_proj = jnp.dot(block_rows, up_weight, preferred_element_type=jnp.float32)
        hidden = (jax.nn.silu(gate_proj) * up_proj).astype(jnp.bfloat16)
        pieces = jnp.einsum('rsf,sfd->srd', hidden.reshape(N_EXPERT * CAP, N_TENSOR, FF_PART).astype(jnp.float32), down_weight.reshape(N_TENSOR, FF_PART, D).astype(jnp.float32))
        rounded = lax.optimization_barrier(pieces.astype(jnp.bfloat16)).astype(jnp.float32)
        expert_sum = lax.optimization_barrier(jnp.sum(rounded, axis=0))
        mixed = mixed.at[indices].add(scales[:, None] * expert_sum, mode='drop')
        return (mixed, None)
    mixed = lax.scan(one_expert, jnp.zeros((TOKENS, D), jnp.float32), (w_gate, w_up, w_down, token_table, weight_table))[0]
    thinker_out = mixed.astype(jnp.bfloat16)
    handed = jnp.dot(thinker_out[source_rows], w_handover, preferred_element_type=jnp.float32).astype(jnp.bfloat16)
    talker_in = handed.astype(jnp.float32) + codec_embeds.astype(jnp.float32)
    talker_normed = rms_scale(talker_in, talker_gain).astype(jnp.bfloat16)
    queries = jnp.dot(talker_normed, w_query, preferred_element_type=jnp.float32)
    key_value = jnp.dot(talker_normed, w_kv, preferred_element_type=jnp.float32)
    group_size = HEADS // KV_HEADS
    query_heads = rms_scale(queries.reshape(N_EXPERT, GROUP_FRAMES, KV_HEADS, group_size, HEAD), qk_gains[0]).astype(jnp.bfloat16)
    key_heads = rms_scale(key_value[:, :KV_HEADS * HEAD].reshape(N_EXPERT, GROUP_FRAMES, KV_HEADS, HEAD), qk_gains[1]).astype(jnp.bfloat16)
    value_heads = key_value[:, KV_HEADS * HEAD:].astype(jnp.bfloat16).reshape(N_EXPERT, GROUP_FRAMES, KV_HEADS, HEAD)
    positions = jnp.arange(GROUP_FRAMES, dtype=jnp.int32)
    first_length = frame_lengths.reshape(N_EXPERT, 2)[:, 0]

    def one_group(inputs):
        query_block, key_block, value_block, split = inputs
        scores = jnp.einsum('fgrh,kgh->grfk', query_block.astype(jnp.float32), key_block.astype(jnp.float32)) * HEAD ** (-0.5)
        later = positions >= split
        allowed = (later[:, None] == later[None, :]) & (positions[None, :] <= positions[:, None])
        masked = jnp.where(allowed[None, None], scores, -jnp.inf)
        row_peak = lax.optimization_barrier(jnp.max(masked, axis=-1, keepdims=True))
        exp_weights = jnp.exp(masked - row_peak).astype(jnp.bfloat16)
        denominator = lax.optimization_barrier(jnp.sum(exp_weights.astype(jnp.float32), axis=-1))
        attended = jnp.einsum('grfk,kgh->fgrh', exp_weights.astype(jnp.float32), value_block.astype(jnp.float32))
        return (attended / jnp.transpose(denominator, (2, 0, 1))[..., None]).astype(jnp.bfloat16)
    attended = lax.map(one_group, (query_heads, key_heads, value_heads, first_length)).reshape(FRAMES, HEADS * HEAD)
    talker_out = jnp.dot(attended, w_out, preferred_element_type=jnp.float32).astype(jnp.bfloat16)
    return (thinker_out, talker_out)
```

```python
import jax
import jax.numpy as jnp
from jax import lax
from jax.sharding import PartitionSpec as P

HEADS = 8
KV_HEADS = 4
HEAD = 128


epsilon = 1e-06


def rms_scale(values, gain):
    mean_square = jnp.mean(values * values, axis=-1, keepdims=True)
    return values * lax.rsqrt(mean_square + epsilon) * gain


def route_slots(expert_ids, expert_count, capacity):
    token_count, top_count = expert_ids.shape
    flat_ids = expert_ids.reshape(token_count * top_count)
    one_hot = (flat_ids[:, None] == jnp.arange(expert_count, dtype=jnp.int32)[None, :]).astype(
        jnp.int32
    )
    before = jnp.cumsum(one_hot, axis=0) - one_hot
    slot_rank = jnp.sum(before * one_hot, axis=1)
    return flat_ids * capacity + slot_rank


def xor_swap(values, axis, mask):
    return lax.ppermute(values, axis, [(i, i ^ mask) for i in range(lax.axis_size(axis))])


def power_of_two(number):
    return number > 0 and number & (number - 1) == 0


def routed_thinker(tokens, norm_gain, expert_ids, route_weights, w_gate, w_up, w_down):
    groups = lax.axis_size("expert")
    tensor_count = lax.axis_size("tensor")
    local_experts = w_gate.shape[0]
    expert_count = local_experts * groups
    token_count, top_count = expert_ids.shape
    capacity = 17 * token_count * top_count // (16 * expert_count)
    model_width = tokens.shape[1]
    slab_width = model_width // tensor_count
    normed = rms_scale(tokens.astype(jnp.float32), norm_gain).astype(jnp.bfloat16)
    padded = jnp.concatenate([normed, jnp.zeros((1, model_width), jnp.bfloat16)], axis=0)
    route_slot = route_slots(expert_ids, expert_count, capacity)
    token_table = jnp.full((expert_count * capacity,), token_count, jnp.int32)
    token_table = token_table.at[route_slot].set(
        jnp.arange(token_count * top_count, dtype=jnp.int32) // top_count
    )
    outgoing = padded[token_table].reshape(groups, local_experts, capacity, model_width)
    received = lax.all_to_all(outgoing, "expert", split_axis=0, concat_axis=0, tiled=True)
    gate_proj = jnp.einsum("secd,edf->secf", received, w_gate, preferred_element_type=jnp.float32)
    up_proj = jnp.einsum("secd,edf->secf", received, w_up, preferred_element_type=jnp.float32)
    hidden = (jax.nn.silu(gate_proj) * up_proj).astype(jnp.bfloat16)
    expert_out = jnp.einsum(
        "secf,efd->secd", hidden, w_down, preferred_element_type=jnp.float32
    ).astype(jnp.bfloat16)
    route_share = route_weights / jnp.sum(route_weights, axis=1, keepdims=True)
    owner_sums = lax.psum_scatter(expert_out, "tensor", scatter_dimension=3, tiled=True)
    returned = lax.all_to_all(owner_sums, "expert", split_axis=0, concat_axis=0, tiled=True)
    picked = returned.reshape(expert_count * capacity, slab_width)[route_slot].reshape(
        token_count, top_count, slab_width
    )
    partial_value = jnp.sum(route_share[:, :, None] * picked.astype(jnp.float32), axis=1)
    return lax.all_to_all(
        partial_value.astype(jnp.bfloat16), "tensor", split_axis=0, concat_axis=1, tiled=True
    )


def gathered_thinker(tokens, norm_gain, expert_ids, route_weights, w_gate, w_up, w_down):
    groups = lax.axis_size("expert")
    far_count = groups // 2
    tensor_index = lax.axis_index("tensor")
    local_experts, model_width, part_width = w_gate.shape
    first_expert = lax.axis_index("expert") * local_experts
    token_count, top_count = expert_ids.shape
    quarter = token_count // lax.axis_size("tensor")
    half = 2 * quarter
    shared = quarter * 3 // 8 // 8 * 8
    direct = quarter + shared
    bf16, f32 = jnp.bfloat16, jnp.float32

    normed = rms_scale(tokens.astype(f32), norm_gain).astype(bf16)
    share = (route_weights / jnp.sum(route_weights, axis=1, keepdims=True)).T
    share_hi = lax.reduce_precision(share, 8, 7)
    info = jnp.concatenate(
        [expert_ids.T.astype(bf16), share_hi.astype(bf16), (share - share_hi).astype(bf16)], axis=0
    )
    info_rows = -(-info.shape[0] * half // model_width)
    info_rows_padded = -(-info_rows // 8) * 8

    def pick(values, lane_flip, axis):
        own = tensor_index ^ lane_flip
        return jnp.concatenate(
            [
                lax.dynamic_slice_in_dim(values, own * quarter, quarter, axis),
                lax.dynamic_slice_in_dim(values, (own ^ 2) * quarter, quarter, axis),
            ],
            axis=axis,
        )

    def unpack(rows):
        flat = rows[direct : direct + info_rows].reshape(-1)
        return flat[: info.shape[0] * half].reshape(info.shape[0], half)

    wide_gate = jnp.transpose(w_gate, (1, 0, 2)).reshape(model_width, local_experts * part_width)
    wide_up = jnp.transpose(w_up, (1, 0, 2)).reshape(model_width, local_experts * part_width)
    wide_down = w_down.reshape(local_experts * part_width, model_width)
    spread = (
        jnp.arange(2 * local_experts, dtype=jnp.int32)[:, None] % local_experts
        == jnp.arange(local_experts * part_width, dtype=jnp.int32)[None, :] // part_width
    ).astype(bf16)

    def experts(rows, row_info):
        ids = row_info[:top_count].astype(f32)
        mine = (first_expert + jnp.arange(local_experts, dtype=jnp.int32)).astype(f32)
        match = ids[None] == mine[:, None, None]
        weights = jnp.concatenate(
            [
                jnp.sum(jnp.where(match, row_info[None, top_count : 2 * top_count].astype(f32), 0.0), axis=1),
                jnp.sum(jnp.where(match, row_info[None, 2 * top_count :].astype(f32), 0.0), axis=1),
            ],
            axis=0,
        ).astype(bf16)
        scale = lax.dot_general(weights, spread, (((0,), (0,)), ((), ())), preferred_element_type=f32)
        gate_proj = jnp.dot(rows, wide_gate, preferred_element_type=f32)
        up_proj = jnp.dot(rows, wide_up, preferred_element_type=f32)
        hidden = (jax.nn.silu(gate_proj) * up_proj * scale).astype(bf16)
        return jnp.dot(hidden, wide_down, preferred_element_type=f32).astype(bf16)

    mine, other = pick(normed, 0, 0), pick(normed, 1, 0)
    mine_info, other_info = pick(info, 0, 1), pick(info, 1, 1)
    flat_info = jnp.pad(
        mine_info.reshape(-1), (0, info_rows_padded * model_width - mine_info.size)
    ).reshape(info_rows_padded, model_width)
    outgoing = jnp.concatenate([mine[:direct], flat_info], axis=0)

    far_rows = [outgoing] + [xor_swap(outgoing, "expert", 2 * j) for j in range(1, far_count)]
    near_rows = [xor_swap(rows, "expert", 1) for rows in far_rows]

    own_out = experts(
        jnp.concatenate([mine, other], axis=0), jnp.concatenate([mine_info, other_info], axis=1)
    )
    sums = []
    for j in range(far_count):
        near_info = unpack(near_rows[j])
        if j == 0:
            side_rows = xor_swap(near_rows[0][shared:quarter], "tensor", 2)
            block = jnp.concatenate([near_rows[0][:direct], side_rows], axis=0)
            block_info = near_info
        else:
            side_rows = xor_swap(
                jnp.concatenate(
                    [far_rows[j][shared:quarter], near_rows[j][shared:quarter]], axis=0
                ),
                "tensor",
                2,
            )
            missing = quarter - shared
            block = jnp.concatenate(
                [
                    far_rows[j][:direct],
                    side_rows[:missing],
                    near_rows[j][:direct],
                    side_rows[missing:],
                ],
                axis=0,
            )
            block_info = jnp.concatenate([unpack(far_rows[j]), near_info], axis=1)
        lane_block = xor_swap(block, "tensor", 1)
        lane_info = xor_swap(block_info, "tensor", 1)
        if j == 0:
            near_out = experts(
                jnp.concatenate([block, lane_block], axis=0),
                jnp.concatenate([block_info, lane_info], axis=1),
            )
            far_sum = own_out[:half].astype(f32) + xor_swap(own_out[half:], "tensor", 1).astype(f32)
            near_sum = near_out[:half].astype(f32) + xor_swap(near_out[half:], "tensor", 1).astype(f32)
        else:
            lane_out = xor_swap(experts(lane_block, lane_info), "tensor", 1)
            both = experts(block, block_info).astype(f32) + lane_out.astype(f32)
            far_sum, near_sum = both[:half], both[half:]
        far_sum, near_sum = far_sum.astype(bf16), near_sum.astype(bf16)
        missing = quarter - shared
        back = xor_swap(
            jnp.concatenate([far_sum[direct:], near_sum[direct:]], axis=0), "tensor", 2
        )

        def with_side(part, extra):
            return jnp.concatenate(
                [
                    part[:shared],
                    (part[shared:quarter].astype(f32) + extra.astype(f32)).astype(bf16),
                    part[quarter:direct],
                ],
                axis=0,
            )

        near_back = xor_swap(with_side(near_sum, back[missing:]), "expert", 1)
        total = (
            with_side(far_sum, back[:missing]).astype(f32) + near_back.astype(f32)
        ).astype(bf16)
        sums.append(total if j == 0 else xor_swap(total, "expert", 2 * j))
    total = sums[0].astype(f32)
    for part in sums[1:]:
        total = total + part.astype(f32)
    last = xor_swap(total[quarter:].astype(bf16), "tensor", 2)
    return jnp.concatenate(
        [total[:shared] + last.astype(f32), total[shared:quarter]], axis=0
    ).astype(bf16)


def gather_tensor(values):
    count = lax.axis_size("tensor")
    order, mask = [0], count // 2
    while mask:
        values = jnp.concatenate([values, xor_swap(values, "tensor", mask)], axis=0)
        order = order + [distance ^ mask for distance in order]
        mask //= 2
    return values, order


def per_device(
    tokens,
    norm_gain,
    expert_ids,
    route_weights,
    w_gate,
    w_up,
    w_down,
    codec_embeds,
    frame_lengths,
    source_rows,
    w_handover,
    talker_gain,
    w_query,
    w_kv,
    qk_gains,
    w_out,
):
    groups = lax.axis_size("expert")
    tensor_count = lax.axis_size("tensor")
    group_index = lax.axis_index("expert")
    tensor_index = lax.axis_index("tensor")
    expert_count = w_gate.shape[0] * groups
    token_count, top_count = expert_ids.shape
    capacity = 17 * token_count * top_count // (16 * expert_count)
    bf16, f32 = jnp.bfloat16, jnp.float32
    gather_all = (
        groups * token_count <= expert_count * capacity
        and power_of_two(groups)
        and groups > 1
        and tensor_count == 4
        and expert_count <= 256
    )
    frames, order = gather_tensor(codec_embeds)
    all_rows, _ = gather_tensor(source_rows)
    thinker = gathered_thinker if gather_all else routed_thinker
    thinker_out = thinker(tokens, norm_gain, expert_ids, route_weights, w_gate, w_up, w_down)

    handed_rows, _ = gather_tensor(
        jnp.dot(thinker_out, w_handover, preferred_element_type=f32).astype(bf16)
    )
    quarter = token_count // tensor_count
    local_rows = all_rows - group_index * token_count
    distance = (local_rows // quarter) ^ tensor_index
    place = jnp.zeros_like(distance)
    for position, value in enumerate(order):
        place = jnp.where(distance == value, position, place)
    local_rows = place * quarter + local_rows % quarter
    picks = (
        local_rows[:, None] == jnp.arange(token_count, dtype=jnp.int32)[None, :]
    ).astype(bf16)
    handed = jnp.dot(picks, handed_rows, preferred_element_type=f32)
    talker_in = handed + frames.astype(f32)
    talker_normed = rms_scale(talker_in, talker_gain).astype(bf16)
    frame_count = codec_embeds.shape[0]
    group_frames = frame_count * tensor_count
    queries = jnp.dot(talker_normed[:frame_count], w_query, preferred_element_type=f32)
    key_value = jnp.dot(talker_normed, w_kv, preferred_element_type=f32)
    group_size = HEADS // KV_HEADS
    query_heads = rms_scale(
        queries.reshape(frame_count, KV_HEADS, group_size, HEAD), qk_gains[0]
    ).astype(bf16)
    group_keys = rms_scale(
        key_value[:, : KV_HEADS * HEAD].reshape(group_frames, KV_HEADS, HEAD), qk_gains[1]
    ).astype(bf16)
    group_values = key_value[:, KV_HEADS * HEAD :].astype(bf16)
    offsets = jnp.arange(frame_count, dtype=jnp.int32)
    key_positions = jnp.concatenate(
        [(tensor_index ^ value) * frame_count + offsets for value in order]
    )
    query_positions = tensor_index * frame_count + offsets
    first_length = frame_lengths[0]
    same_dialog = (query_positions[:, None] >= first_length) == (
        key_positions[None, :] >= first_length
    )
    allowed = same_dialog & (key_positions[None, :] <= query_positions[:, None])
    scores = jnp.einsum(
        "fgrh,kgh->grfk", query_heads, group_keys, preferred_element_type=f32
    ) * HEAD ** (-0.5)
    masked = jnp.where(allowed[None, None], scores, -jnp.inf)
    row_peak = jnp.max(masked, axis=-1, keepdims=True)
    exp_weights = jnp.exp(masked - row_peak).astype(bf16)
    denominator = jnp.sum(exp_weights.astype(f32), axis=-1)
    attended = jnp.einsum(
        "grfk,kgh->fgrh",
        exp_weights,
        group_values.reshape(group_frames, KV_HEADS, HEAD),
        preferred_element_type=f32,
    )
    attended = (
        (attended / jnp.transpose(denominator, (2, 0, 1))[..., None])
        .astype(bf16)
        .reshape(frame_count, HEADS * HEAD)
    )
    talker_out = jnp.dot(attended, w_out, preferred_element_type=f32).astype(bf16)
    return (thinker_out, talker_out)


def solution(mesh):
    placed = (
        P("expert", None),
        P(),
        P("expert", None),
        P("expert", None),
        P("expert", None, "tensor"),
        P("expert", None, "tensor"),
        P("expert", "tensor", None),
        P(("expert", "tensor"), None),
        P("expert"),
        P(("expert", "tensor")),
        P(),
        P(),
        P(),
        P(),
        P(),
        P(),
    )
    return jax.shard_map(
        per_device,
        mesh=mesh,
        in_specs=placed,
        out_specs=(P(("expert", "tensor"), None), P(("expert", "tensor"), None)),
        check_vma=False,
    )
```
